32 devices in a mesh: snap: 16 (over z, y, x), vert: 2 (over core).
Axes of the slice: x: 2, y: 2, z: 4, core: 2. Of those that a mesh axis runs over, the one named last changes fastest.
Arguments:
- features: bfloat16 [32, 2048, 128], P('snap', 'vert'), may hold values from -6 to 6
- tile_cols: int32 [32, 16, 8], P('snap', 'vert'), may hold values from 0 to 15
- tile_weights: int32 [32, 16, 8, 128, 128], P('snap', 'vert'), may hold values from 0 to 3
- graph_gain: float32 [2, 128], replicated, may hold values from 0.5 to 1.5
- graph_up: bfloat16 [2, 128, 512], replicated, may hold values from -0.5 to 0.5
- graph_down: bfloat16 [2, 512, 128], replicated, may hold values from -0.25 to 0.25
- lag_mix: float32 [2, 8, 128], replicated, may hold values from -2 to 2
- time_gain: float32 [2, 128], replicated, may hold values from 0.5 to 1.5
- time_up: bfloat16 [2, 128, 1024], replicated, may hold values from -0.5 to 0.5
- time_down: bfloat16 [2, 1024, 128], replicated, may hold values from -0.1875 to 0.1875
Outputs:
- result: bfloat16 [32, 2048, 128], P('snap', 'vert')
The draws below stay inside these ranges and needn't reach their ends.
All inputs are finite; a program needn't handle non-finite values.
Results may differ from the reference program's by a relative error of at most 0.0085.
Values may be sent and summed in bfloat16 or wider, within the bound.
A program may use at most 64 MiB of HBM per device.

```python
import jax
import jax.numpy as jnp
from jax import lax

F = 128
HG = 512
HT = 1024
TILE = 128
K = 8
LAGS = 8
LAYERS = 2
SNAPS = 32
VERTS = 2048


def with_ends(drawn, stream_key, least, high):
    spot = [jax.random.randint(jax.random.fold_in(stream_key, axis), (), 0, length) for axis, length in enumerate(drawn.shape)]
    longest = drawn.shape.index(max(drawn.shape))
    neighbour = spot[:longest] + [(spot[longest] + 1) % drawn.shape[longest]] + spot[longest + 1:]
    return drawn.at[tuple(spot)].set(least).at[tuple(neighbour)].set(high)


def block_levels(rng, shape, split, low, high):
    def one(position, blocks):
        heights = jax.random.uniform(jax.random.fold_in(jax.random.fold_in(rng, 6), position), (blocks,), jnp.float32, low / len(split), high / len(split))
        return jnp.repeat(jnp.exp(heights), shape[position] // blocks).reshape((-1,) + (1,) * (len(shape) - position - 1))

    gain = one(*split[0])
    for cut in split[1:]:
        gain = gain * one(*cut)
    return gain


def gaussian(key, extent, scale, bound, pieces=(), held_as=jnp.bfloat16):
    drawn = jax.random.normal(key, extent, jnp.float32) * scale
    if len(pieces) > 0:
        drawn = block_levels(key, extent, pieces, -0.22, 0.18) * drawn
    return jnp.clip(drawn, min=-bound, max=bound).astype(held_as)


def setup_inputs(seed: int = 0) -> dict:
    key_of = jax.random.split(jax.random.key(seed), 11)
    features = gaussian(key_of[0], (SNAPS, VERTS, F), 1.0, 6.0, ((0, 16), (1, 2)))
    tile_cols = with_ends(jax.random.randint(key_of[1], (SNAPS, VERTS // TILE, K), 0, VERTS // TILE), jax.random.fold_in(key_of[1], 1), 0, (VERTS // TILE) - 1).astype(jnp.int32)
    tile_weights = with_ends(jax.random.randint(key_of[2], (SNAPS, VERTS // TILE, K, TILE, TILE), 0, 4), jax.random.fold_in(key_of[2], 1), 0, 3).astype(jnp.int32)
    graph_gain = jnp.clip(1.0 + 0.1 * jax.random.normal(key_of[3], (LAYERS, F), jnp.float32), 0.5, 1.5)
    graph_up = gaussian(key_of[4], (LAYERS, F, HG), F ** -0.5, 0.5)
    graph_down = gaussian(key_of[5], (LAYERS, HG, F), HG ** -0.5, 0.25)
    lag_mix = gaussian(key_of[6], (LAYERS, LAGS, F), LAGS ** -0.5, 2.0, (), jnp.float32)
    time_gain = jnp.clip(1.0 + 0.1 * jax.random.normal(key_of[7], (LAYERS, F), jnp.float32), 0.5, 1.5)
    time_up = gaussian(key_of[8], (LAYERS, F, HT), F ** -0.5, 0.5)
    time_down = gaussian(key_of[9], (LAYERS, HT, F), HT ** -0.5, 0.1875)
    return dict(features=features, tile_cols=tile_cols, tile_weights=tile_weights, graph_gain=graph_gain, graph_up=graph_up, graph_down=graph_down, lag_mix=lag_mix, time_gain=time_gain, time_up=time_up, time_down=time_down)


eps = 1e-06

def rms_scale(activation, gain_row):
    return activation * lax.rsqrt(lax.optimization_barrier(jnp.mean(activation * activation, axis=-1, keepdims=True)) + eps) * gain_row

def mlp_branch(residual, mixed_rows, gain_row, up_weight, down_weight):
    feature_width = residual.shape[-1]
    normed = rms_scale(mixed_rows, gain_row).astype(jnp.bfloat16).reshape(-1, feature_width)
    hidden = jax.nn.gelu(jnp.dot(normed, up_weight, preferred_element_type=jnp.float32)).astype(jnp.bfloat16)
    branch = jnp.dot(hidden, down_weight, preferred_element_type=jnp.float32).reshape(residual.shape)
    return (residual.astype(jnp.float32) + branch).astype(jnp.bfloat16)

def lagged(sequence, lag_rows, before, out_count):
    widened = sequence.astype(jnp.float32)
    running = jnp.zeros((out_count,) + sequence.shape[1:], jnp.float32)
    for lag_step in range(lag_rows.shape[0]):
        running = running + lag_rows[lag_step] * lax.slice_in_dim(widened, before - lag_step, before - lag_step + out_count, axis=0)
    return running

def aggregate(snapshot, columns, blocks):
    feature_width = snapshot.shape[-1]
    stacked = snapshot.reshape(-1, TILE, feature_width)
    picked = stacked[columns]
    product = jnp.einsum('rkij,rkjf->rif', blocks.astype(jnp.float32), picked.astype(jnp.float32))
    return product.reshape(-1, feature_width)

def reference(features, tile_cols, tile_weights, graph_gain, graph_up, graph_down, lag_mix, time_gain, time_up, time_down):
    state = features
    for layer_index in range(LAYERS):

        def one_snapshot(operands):
            return aggregate(operands[0], operands[1], operands[2])
        summed = lax.map(one_snapshot, (state, tile_cols, tile_weights))
        graph_out = mlp_branch(state, summed, graph_gain[layer_index], graph_up[layer_index], graph_down[layer_index])
        padded = jnp.concatenate([jnp.zeros((LAGS - 1,) + graph_out.shape[1:], jnp.bfloat16), graph_out], axis=0)
        mixed_rows = lagged(padded, lag_mix[layer_index], LAGS - 1, SNAPS)
        state = mlp_branch(graph_out, mixed_rows, time_gain[layer_index], time_up[layer_index], time_down[layer_index])
    return state
```

```python
import functools

import jax
import jax.numpy as jnp
from jax import lax
from jax.experimental import pallas as pl
from jax.experimental.pallas import tpu as pltpu
from jax.sharding import PartitionSpec as P

eps = 1e-06
MESH = pl.DeviceIdType.MESH


def normalise(rows, gain_row):
    scale = lax.rsqrt(jnp.mean(rows * rows, axis=-1, keepdims=True) + eps)
    return (rows * scale * gain_row).astype(jnp.bfloat16)


def mlp(normed, up_weight, down_weight):
    hidden = jnp.dot(normed, up_weight, preferred_element_type=jnp.float32)
    hidden = jax.nn.gelu(hidden).astype(jnp.bfloat16)
    return jnp.dot(hidden, down_weight, preferred_element_type=jnp.float32)


def kernel(
    owners, verts, group,
    feats, cols, weights, graph_gain, graph_up, graph_down, lag_mix, time_gain, time_up, time_down,
    out, *scratch,
):
    layers = lag_mix.shape[0]
    full = scratch[:layers]
    (
        raw, blocks, sent_graph, window, sent_time,
        raw_sem, first_send, first_recv, a_send, a_recv, z_send, z_recv, b_send, b_recv, v_send, v_recv,
    ) = scratch[layers:]
    snaps, tiles, tile, width = feats.shape
    picks = weights.shape[2]
    lags = lag_mix.shape[1]
    chunks = tiles // group
    held = group * snaps
    groups = owners // group

    me = lax.axis_index("snap")
    core = lax.axis_index("vert")
    slot = me % group
    plane = me // group
    base = me - slot
    first_tile = core * tiles

    def raw_copy(r):
        return pltpu.make_async_copy(weights.at[:, r], raw.at[:, r], raw_sem.at[r])

    for r in range(tiles):
        raw_copy(r).start()

    barrier = pltpu.get_barrier_semaphore()
    for d in range(1, group):
        pl.semaphore_signal(barrier, inc=1, device_id=(base + (slot + d) % group, core), device_id_type=MESH)
    for q in range(1, verts):
        pl.semaphore_signal(barrier, inc=1, device_id=(me, (core + q) % verts), device_id_type=MESH)

    @pl.when(plane > 0)
    def _():
        pl.semaphore_signal(barrier, inc=1, device_id=(me - group, core), device_id_type=MESH)

    @pl.when(plane < groups - 1)
    def _():
        pl.semaphore_signal(barrier, inc=1, device_id=(me + group, core), device_id_type=MESH)

    ahead = jnp.where(plane < groups - 1, 1, 0)
    behind = jnp.where(plane > 0, 1, 0)
    pl.semaphore_wait(barrier, group - 1 + verts - 1 + ahead + behind)

    def first_copy(q):
        return pltpu.make_async_remote_copy(
            src_ref=feats,
            dst_ref=full[0].at[:, pl.ds(first_tile, tiles)],
            send_sem=first_send.at[q],
            recv_sem=first_recv.at[q],
            device_id=(me, (core + q) % verts),
            device_id_type=MESH,
        )

    for q in range(1, verts):
        first_copy(q).start()

    full[0][:, pl.ds(first_tile, tiles)] = feats[...]

    @pl.when(plane == 0)
    def _():
        for l in range(layers):
            for h in range(chunks):
                window[l, h, 0:held] = jnp.zeros((held, tile, width), jnp.bfloat16)

    def convert(r, carry):
        raw_copy(r).wait()
        for t in range(snaps):
            for k in range(picks):
                blocks[t, r, :, k * tile:(k + 1) * tile] = raw[t, r, k].astype(jnp.float32).astype(jnp.bfloat16)
        return carry

    lax.fori_loop(0, tiles, convert, 0)

    for q in range(1, verts):
        first_copy(q).wait_recv()

    def a_copy(l, h, d):
        return pltpu.make_async_remote_copy(
            src_ref=sent_graph.at[l, h, d],
            dst_ref=window.at[l, h, pl.ds(held + slot * snaps, snaps)],
            send_sem=a_send.at[l, h, d],
            recv_sem=a_recv.at[l, h, d],
            device_id=(base + (slot + d) % group, core),
            device_id_type=MESH,
        )

    def z_copy(l, h, d):
        origin = ((slot + group - d) % group) * snaps
        return pltpu.make_async_remote_copy(
            src_ref=window.at[l, h, pl.ds(held + origin, snaps)],
            dst_ref=window.at[l, h, pl.ds(origin, snaps)],
            send_sem=z_send.at[l, h, d],
            recv_sem=z_recv.at[l, h, d],
            device_id=(jnp.minimum(me + group, owners - 1), core),
            device_id_type=MESH,
        )

    def b_copy(l, h, d):
        place = slot * chunks + h
        return pltpu.make_async_remote_copy(
            src_ref=sent_time.at[l, h, d],
            dst_ref=out.at[:, place] if l == layers - 1 else full[l + 1].at[:, first_tile + place],
            send_sem=b_send.at[l, h, d],
            recv_sem=b_recv.at[l, h, d],
            device_id=(base + (slot + d) % group, core),
            device_id_type=MESH,
        )

    def v_copy(l, h, d, q):
        piece = full[l + 1].at[:, first_tile + ((slot + group - d) % group) * chunks + h]
        return pltpu.make_async_remote_copy(
            src_ref=piece,
            dst_ref=piece,
            send_sem=v_send.at[l, h, d, q],
            recv_sem=v_recv.at[l, h, d, q],
            device_id=(me, (core + q) % verts),
            device_id_type=MESH,
        )

    def hand_on(l, h, d):
        @pl.when(plane < groups - 1)
        def _():
            z_copy(l, h, d).start()

    def share(l, h, d):
        if l < layers - 1:
            for q in range(1, verts):
                v_copy(l, h, d, q).start()

    for l in range(layers):

        def graph_step(step, carry):
            h, d = step // group, step % group
            r = ((slot + d) % group) * chunks + h
            sums = []
            for t in range(snaps):
                picked = jnp.concatenate([full[l][t, cols[t, r, k]] for k in range(picks)], axis=0)
                sums.append(jnp.dot(blocks[t, r], picked, preferred_element_type=jnp.float32))
            summed = jnp.concatenate(sums, axis=0)
            branch = mlp(normalise(summed, graph_gain[l:l + 1]), graph_up[l], graph_down[l])
            state = full[l][:, first_tile + r].astype(jnp.float32)
            result = (state + branch.reshape(snaps, tile, width)).astype(jnp.bfloat16)

            @pl.when(d == 0)
            def _():
                window[l, h, pl.ds(held + slot * snaps, snaps)] = result
                hand_on(l, h, d)

            @pl.when(d > 0)
            def _():
                sent_graph[l, h, d] = result
                a_copy(l, h, d).start()

                @pl.when(h > 0)
                def _():
                    a_copy(l, h - 1, d).wait_recv()
                    hand_on(l, h - 1, d)

            return carry

        lax.fori_loop(0, chunks * group, graph_step, 0)
        for d in range(1, group):
            a_copy(l, chunks - 1, d).wait_recv()
            hand_on(l, chunks - 1, d)

        def time_step(step, carry):
            h, d = step // group, (step + 1) % group

            @pl.when(jnp.logical_and(d == 1 % group, plane > 0))
            def _():
                for e in range(group):
                    z_copy(l, h, e).wait_recv()

            owner = (slot + d) % group
            rows = []
            for t in range(snaps):
                newest = held + owner * snaps + t
                mixed = lag_mix[l, 0:1] * window[l, h, newest].astype(jnp.float32)
                for m in range(1, lags):
                    mixed = mixed + lag_mix[l, m:m + 1] * window[l, h, newest - m].astype(jnp.float32)
                rows.append(mixed)
            mixed = jnp.concatenate(rows, axis=0)
            branch = mlp(normalise(mixed, time_gain[l:l + 1]), time_up[l], time_down[l])
            state = window[l, h, pl.ds(held + owner * snaps, snaps)].astype(jnp.float32)
            result = (state + branch.reshape(snaps, tile, width)).astype(jnp.bfloat16)

            @pl.when(d == 0)
            def _():
                place = slot * chunks + h
                if l == layers - 1:
                    out[:, place] = result
                else:
                    full[l + 1][:, first_tile + place] = result
                    share(l, h, d)

            @pl.when(d > 0)
            def _():
                sent_time[l, h, d] = result
                b_copy(l, h, d).start()

                @pl.when(h > 0)
                def _():
                    b_copy(l, h - 1, d).wait_recv()
                    share(l, h - 1, d)

            return carry

        lax.fori_loop(0, chunks * group, time_step, 0)
        for d in range(1, group):
            b_copy(l, chunks - 1, d).wait_recv()
            share(l, chunks - 1, d)
        if l < layers - 1:
            for h in range(chunks):
                for d in range(group):
                    for q in range(1, verts):
                        v_copy(l, h, d, q).wait_recv()

    for q in range(1, verts):
        first_copy(q).wait_send()
    for l in range(layers):
        for h in range(chunks):
            for d in range(1, group):
                a_copy(l, h, d).wait_send()
                b_copy(l, h, d).wait_send()
            for d in range(group):
                if l < layers - 1:
                    for q in range(1, verts):
                        v_copy(l, h, d, q).wait_send()

                @pl.when(plane < groups - 1)
                def _():
                    z_copy(l, h, d).wait_send()


def on_device(owners, verts, features, tile_cols, tile_weights, graph_gain, graph_up, graph_down, lag_mix, time_gain, time_up, time_down):
    snaps, vert_dev, width = features.shape
    _, tiles, picks, tile, _ = tile_weights.shape
    layers, lags = lag_mix.shape[0], lag_mix.shape[1]
    group = -(-(lags - 1) // snaps)
    while owners % group or tiles % group:
        group += 1
    chunks = tiles // group
    held = group * snaps
    vmem = pl.BlockSpec(memory_space=pltpu.VMEM)
    bf16 = jnp.bfloat16
    dma = pltpu.SemaphoreType.DMA
    result = pl.pallas_call(
        functools.partial(kernel, owners, verts, group),
        out_shape=jax.ShapeDtypeStruct((snaps, tiles, tile, width), bf16),
        in_specs=[
            vmem,
            pl.BlockSpec(memory_space=pltpu.SMEM),
            pl.BlockSpec(memory_space=pl.ANY),
        ] + [vmem] * 7,
        out_specs=vmem,
        scratch_shapes=[pltpu.VMEM((snaps, verts * tiles, tile, width), bf16)] * layers + [
            pltpu.VMEM((snaps, tiles, picks, tile, tile), jnp.int32),
            pltpu.VMEM((snaps, tiles, tile, picks * tile), bf16),
            pltpu.VMEM((layers, chunks, group, snaps, tile, width), bf16),
            pltpu.VMEM((layers, chunks, 2 * held, tile, width), bf16),
            pltpu.VMEM((layers, chunks, group, snaps, tile, width), bf16),
            dma((tiles,)),
            dma((verts,)),
            dma((verts,)),
        ] + [dma((layers, chunks, group))] * 6 + [dma((layers, chunks, group, verts))] * 2,
        compiler_params=pltpu.CompilerParams(
            collective_id=0, has_side_effects=True, vmem_limit_bytes=60 * 1024 * 1024
        ),
    )(
        features.reshape(snaps, tiles, tile, width), tile_cols, tile_weights,
        graph_gain, graph_up, graph_down, lag_mix, time_gain, time_up, time_down,
    )
    return result.reshape(features.shape)


def solution(mesh):
    return jax.shard_map(
        functools.partial(on_device, mesh.shape["snap"], mesh.shape["vert"]),
        mesh=mesh,
        in_specs=(
            P("snap", "vert", None),
            P("snap", "vert", None),
            P("snap", "vert", None, None, None),
        ) + (P(),) * 7,
        out_specs=P("snap", "vert", None),
        check_vma=False,
    )
```

```python
import functools

import jax
import jax.numpy as jnp
from jax import lax
from jax.experimental import pallas as pl
from jax.experimental.pallas import tpu as pltpu
from jax.sharding import PartitionSpec as P

eps = 1e-06
MESH = pl.DeviceIdType.MESH


def normalise(rows, gain_row):
    scale = lax.rsqrt(jnp.mean(rows * rows, axis=-1, keepdims=True) + eps)
    return (rows * scale * gain_row).astype(jnp.bfloat16)


def mlp(normed, up_weight, down_weight):
    hidden = jnp.dot(normed, up_weight, preferred_element_type=jnp.float32)
    hidden = jax.nn.gelu(hidden).astype(jnp.bfloat16)
    return jnp.dot(hidden, down_weight, preferred_element_type=jnp.float32)


def kernel(
    owners, verts, group,
    feats, cols, weights, graph_gain, lag_mix, time_gain, graph_up_far, graph_down_far, time_up_far, time_down_far,
    out, *scratch,
):
    layers = lag_mix.shape[0]
    full = scratch[:layers]
    (
        raw, blocks, sent_graph, window, sent_time,
        graph_up, graph_down, time_up, time_down, own_sem, far_sem, raw_sem, first_send, first_recv, a_send, a_recv, z_send, z_recv, b_send, b_recv, v_send, v_recv,
    ) = scratch[layers:]
    snaps, tiles, tile, width = feats.shape
    picks = weights.shape[2]
    lags = lag_mix.shape[1]
    chunks = tiles // group
    rows = window.shape[3]
    parts = tile // rows
    pieces = chunks * parts
    held = group * snaps
    unused = min(held - (lags - 1), snaps - 1)
    pair = 2 if group % 2 == 0 else 1
    groups = owners // group

    me = lax.axis_index("snap")
    core = lax.axis_index("vert")
    slot = me % group
    plane = me // group
    base = me - slot
    first_tile = core * tiles

    def far_copy(i, l):
        far, near = (
            (graph_up_far, graph_up), (graph_down_far, graph_down), (time_up_far, time_up), (time_down_far, time_down)
        )[i]
        return pltpu.make_async_copy(far.at[l], near.at[l], far_sem.at[i, l])

    def raw_copy(r):
        return pltpu.make_async_copy(weights.at[:, r], raw.at[:, r], raw_sem.at[r])

    own_copy = pltpu.make_async_copy(feats, full[0].at[:, pl.ds(first_tile, tiles)], own_sem)
    own_copy.start()
    for i in range(2):
        far_copy(i, 0).start()
    for h in range(chunks):
        for d in range(group):
            raw_copy(((slot + d) % group) * chunks + h).start()
    for l in range(layers):
        for i in range(4):
            if l > 0 or i > 1:
                far_copy(i, l).start()

    barrier = pltpu.get_barrier_semaphore()
    for d in range(1, group):
        pl.semaphore_signal(barrier, inc=1, device_id=(base + (slot + d) % group, core), device_id_type=MESH)
    for q in range(1, verts):
        pl.semaphore_signal(barrier, inc=1, device_id=(me, (core + q) % verts), device_id_type=MESH)

    @pl.when(plane > 0)
    def _():
        pl.semaphore_signal(barrier, inc=1, device_id=(me - group, core), device_id_type=MESH)

    @pl.when(plane < groups - 1)
    def _():
        pl.semaphore_signal(barrier, inc=1, device_id=(me + group, core), device_id_type=MESH)

    ahead = jnp.where(plane < groups - 1, 1, 0)
    behind = jnp.where(plane > 0, 1, 0)
    pl.semaphore_wait(barrier, group - 1 + verts - 1 + ahead + behind)

    def first_copy(q):
        return pltpu.make_async_remote_copy(
            src_ref=feats,
            dst_ref=full[0].at[:, pl.ds(first_tile, tiles)],
            send_sem=first_send.at[q],
            recv_sem=first_recv.at[q],
            device_id=(me, (core + q) % verts),
            device_id_type=MESH,
        )

    for q in range(1, verts):
        first_copy(q).start()

    @pl.when(plane == 0)
    def _():
        for l in range(layers):
            for h in range(pieces):
                window[l, h, 0:held] = jnp.zeros((held, rows, width), jnp.bfloat16)

    own_copy.wait()
    for q in range(1, verts):
        first_copy(q).wait_recv()

    def a_copy(l, h, d):
        return pltpu.make_async_remote_copy(
            src_ref=sent_graph.at[l, h, d],
            dst_ref=window.at[l, h, pl.ds(held + slot * snaps, snaps)],
            send_sem=a_send.at[l, h, d],
            recv_sem=a_recv.at[l, h, d],
            device_id=(base + (slot + d) % group, core),
            device_id_type=MESH,
        )

    def z_part(l, h, d, origin, skip):
        return pltpu.make_async_remote_copy(
            src_ref=window.at[l, h, pl.ds(held + origin * snaps + skip, snaps - skip)],
            dst_ref=window.at[l, h, pl.ds(origin * snaps + skip, snaps - skip)],
            send_sem=z_send.at[l, h, d],
            recv_sem=z_recv.at[l, h, d],
            device_id=(jnp.minimum(me + group, owners - 1), core),
            device_id_type=MESH,
        )

    def z_do(l, h, d, act):
        origin = (slot + group - d) % group
        if unused == 0:
            act(z_part(l, h, d, origin, 0))
            return

        @pl.when(origin == 0)
        def _():
            act(z_part(l, h, d, 0, unused))

        @pl.when(origin > 0)
        def _():
            act(z_part(l, h, d, origin, 0))

    def spot(l, owner, h):
        target = out if l == layers - 1 else full[l + 1]
        first = 0 if l == layers - 1 else first_tile
        return target.at[:, first + owner * chunks + h // parts, pl.ds((h % parts) * rows, rows)]

    def b_copy(l, h, d):
        return pltpu.make_async_remote_copy(
            src_ref=sent_time.at[l, h, d],
            dst_ref=spot(l, slot, h),
            send_sem=b_send.at[l, h, d],
            recv_sem=b_recv.at[l, h, d],
            device_id=(base + (slot + d) % group, core),
            device_id_type=MESH,
        )

    def v_copy(l, h, d, q):
        piece = spot(l, (slot + group - d) % group, h)
        return pltpu.make_async_remote_copy(
            src_ref=piece,
            dst_ref=piece,
            send_sem=v_send.at[l, h, d, q],
            recv_sem=v_recv.at[l, h, d, q],
            device_id=(me, (core + q) % verts),
            device_id_type=MESH,
        )

    def hand_on(l, h, d):
        @pl.when(plane < groups - 1)
        def _():
            z_do(l, h, d, lambda copy: copy.start())

    def share(l, h, d):
        if l < layers - 1:
            for q in range(1, verts):
                v_copy(l, h, d, q).start()

    for l in range(layers):
        for i in range(2):
            far_copy(i, l).wait()

        def graph_step(step, carry):
            h, d = step // group, step % group
            r = ((slot + d) % group) * chunks + h
            if l == 0:
                raw_copy(r).wait()
            sums = []
            for t in range(snaps):
                if l == 0:
                    block = jnp.concatenate(
                        [raw[t, r, k].astype(jnp.float32).astype(jnp.bfloat16) for k in range(picks)], axis=1
                    )
                    blocks[t, r] = block
                else:
                    block = blocks[t, r]
                picked = jnp.concatenate([full[l][t, cols[t, r, k]] for k in range(picks)], axis=0)
                sums.append(jnp.dot(block, picked, preferred_element_type=jnp.float32))
            summed = jnp.concatenate(sums, axis=0)
            branch = mlp(normalise(summed, graph_gain[l:l + 1]), graph_up[l], graph_down[l])
            state = full[l][:, first_tile + r].astype(jnp.float32)
            result = (state + branch.reshape(snaps, tile, width)).astype(jnp.bfloat16)

            @pl.when(d == 0)
            def _():
                for p in range(parts):
                    window[l, h * parts + p, pl.ds(held + slot * snaps, snaps)] = result[:, p * rows:(p + 1) * rows]
                    hand_on(l, h * parts + p, d)

            @pl.when(d > 0)
            def _():
                for p in range(parts):
                    sent_graph[l, h * parts + p, d] = result[:, p * rows:(p + 1) * rows]
                    a_copy(l, h * parts + p, d).start()

                @pl.when(h > 0)
                def _():
                    for p in range(parts):
                        a_copy(l, (h - 1) * parts + p, d).wait_recv()
                        hand_on(l, (h - 1) * parts + p, d)

            return carry

        lax.fori_loop(0, chunks * group, graph_step, 0)
        for p in range(parts):
            for d in range(1, group):
                a_copy(l, pieces - parts + p, d).wait_recv()
                hand_on(l, pieces - parts + p, d)
        for i in range(2, 4):
            far_copy(i, l).wait()

        def time_step(step, carry):
            h, first = step // (group // pair), (step % (group // pair)) * pair

            @pl.when(jnp.logical_and(first == 0, plane > 0))
            def _():
                for e in range(group):
                    z_do(l, h, e, lambda copy: copy.wait_recv())

            mixes, states = [], []
            for c in range(pair):
                owner = (slot + first + c + 1) % group
                for t in range(snaps):
                    newest = held + owner * snaps + t
                    mixed = lag_mix[l, 0:1] * window[l, h, newest].astype(jnp.float32)
                    for m in range(1, lags):
                        mixed = mixed + lag_mix[l, m:m + 1] * window[l, h, newest - m].astype(jnp.float32)
                    mixes.append(mixed)
                    states.append(window[l, h, newest].astype(jnp.float32))
            branch = mlp(normalise(jnp.concatenate(mixes, axis=0), time_gain[l:l + 1]), time_up[l], time_down[l])
            result = (jnp.concatenate(states, axis=0) + branch).astype(jnp.bfloat16)
            result = result.reshape(pair, snaps, rows, width)

            for c in range(pair):
                d = (first + c + 1) % group

                def keep(c=c, d=d):
                    spot(l, slot, h)[...] = result[c]
                    share(l, h, d)

                def send(c=c, d=d):
                    sent_time[l, h, d] = result[c]
                    b_copy(l, h, d).start()

                    @pl.when(h > 0)
                    def _():
                        b_copy(l, h - 1, d).wait_recv()
                        share(l, h - 1, d)

                pl.when(d == 0)(keep)
                pl.when(d > 0)(send)

            return carry

        lax.fori_loop(0, pieces * (group // pair), time_step, 0)
        for d in range(1, group):
            b_copy(l, pieces - 1, d).wait_recv()
            share(l, pieces - 1, d)
        if l < layers - 1:
            for h in range(pieces):
                for d in range(group):
                    for q in range(1, verts):
                        v_copy(l, h, d, q).wait_recv()

    for q in range(1, verts):
        first_copy(q).wait_send()
    for l in range(layers):
        for h in range(pieces):
            for d in range(1, group):
                a_copy(l, h, d).wait_send()
                b_copy(l, h, d).wait_send()
            for d in range(group):
                if l < layers - 1:
                    for q in range(1, verts):
                        v_copy(l, h, d, q).wait_send()

                @pl.when(plane < groups - 1)
                def _():
                    z_do(l, h, d, lambda copy: copy.wait_send())


def on_device(owners, verts, features, tile_cols, tile_weights, graph_gain, graph_up, graph_down, lag_mix, time_gain, time_up, time_down):
    snaps, vert_dev, width = features.shape
    _, tiles, picks, tile, _ = tile_weights.shape
    layers, lags = lag_mix.shape[0], lag_mix.shape[1]
    group = -(-(lags - 1) // snaps)
    while owners % group or tiles % group:
        group += 1
    rows = tile // 2
    pieces = tiles // group * 2
    held = group * snaps
    vmem = pl.BlockSpec(memory_space=pltpu.VMEM)
    far = pl.BlockSpec(memory_space=pl.ANY)
    bf16 = jnp.bfloat16
    dma = pltpu.SemaphoreType.DMA
    result = pl.pallas_call(
        functools.partial(kernel, owners, verts, group),
        out_shape=jax.ShapeDtypeStruct((snaps, tiles, tile, width), bf16),
        in_specs=[far, pl.BlockSpec(memory_space=pltpu.SMEM), far, vmem, vmem, vmem] + [far] * 4,
        out_specs=vmem,
        scratch_shapes=[pltpu.VMEM((snaps, verts * tiles, tile, width), bf16)] * layers + [
            pltpu.VMEM((snaps, tiles, picks, tile, tile), jnp.int32),
            pltpu.VMEM((snaps, tiles, tile, picks * tile), bf16),
            pltpu.VMEM((layers, pieces, group, snaps, rows, width), bf16),
            pltpu.VMEM((layers, pieces, 2 * held, rows, width), bf16),
            pltpu.VMEM((layers, pieces, group, snaps, rows, width), bf16),
            pltpu.VMEM(graph_up.shape, bf16),
            pltpu.VMEM(graph_down.shape, bf16),
            pltpu.VMEM(time_up.shape, bf16),
            pltpu.VMEM(time_down.shape, bf16),
            dma,
            dma((4, layers)),
            dma((tiles,)),
            dma((verts,)),
            dma((verts,)),
        ] + [dma((layers, pieces, group))] * 6 + [dma((layers, pieces, group, verts))] * 2,
        compiler_params=pltpu.CompilerParams(
            collective_id=0, has_side_effects=True, vmem_limit_bytes=60 * 1024 * 1024
        ),
    )(
        features.reshape(snaps, tiles, tile, width), tile_cols, tile_weights,
        graph_gain, lag_mix, time_gain, graph_up, graph_down, time_up, time_down,
    )
    return result.reshape(features.shape)


def solution(mesh):
    return jax.shard_map(
        functools.partial(on_device, mesh.shape["snap"], mesh.shape["vert"]),
        mesh=mesh,
        in_specs=(
            P("snap", "vert", None),
            P("snap", "vert", None),
            P("snap", "vert", None, None, None),
        ) + (P(),) * 7,
        out_specs=P("snap", "vert", None),
        check_vma=False,
    )
```

```python
import functools

import jax
import jax.numpy as jnp
from jax import lax
from jax.experimental import pallas as pl
from jax.experimental.pallas import tpu as pltpu
from jax.sharding import PartitionSpec as P

eps = 1e-06
MESH = pl.DeviceIdType.MESH


def normalise(rows, gain_row):
    scale = lax.rsqrt(jnp.mean(rows * rows, axis=-1, keepdims=True) + eps)
    return (rows * scale * gain_row).astype(jnp.bfloat16)


def mlp(normed, up_weight, down_weight):
    hidden = jnp.dot(normed, up_weight, preferred_element_type=jnp.float32)
    hidden = jax.nn.gelu(hidden.astype(jnp.bfloat16))
    return jnp.dot(hidden, down_weight, preferred_element_type=jnp.float32)


def kernel(
    owners, verts, group,
    feats, cols, weights, graph_gain, lag_mix, time_gain, graph_up_far, graph_down_far, time_up_far, time_down_far,
    out, *scratch,
):
    layers = lag_mix.shape[0]
    full = scratch[:layers]
    (
        raw, blocks, sent_graph, window, sent_time,
        graph_up, graph_down, time_up, time_down, own_sem, far_sem, raw_sem, first_send, first_recv, a_send, a_recv, z_send, z_recv, b_send, b_recv, v_send, v_recv,
    ) = scratch[layers:]
    snaps, tiles, tile, width = feats.shape
    picks = weights.shape[2]
    lags = lag_mix.shape[1]
    chunks = tiles // group
    rows = window.shape[3]
    parts = tile // rows
    pieces = chunks * parts
    held = group * snaps
    unused = min(held - (lags - 1), snaps - 1)
    pair = 2 if group % 2 == 0 else 1
    groups = owners // group

    me = lax.axis_index("snap")
    core = lax.axis_index("vert")
    slot = me % group
    plane = me // group
    base = me - slot
    first_tile = core * tiles

    def far_copy(i, l):
        far, near = (
            (graph_up_far, graph_up), (graph_down_far, graph_down), (time_up_far, time_up), (time_down_far, time_down)
        )[i]
        return pltpu.make_async_copy(far.at[l], near.at[l], far_sem.at[i, l])

    def raw_copy(r):
        return pltpu.make_async_copy(weights.at[:, r], raw.at[:, r], raw_sem.at[r])

    own_copy = pltpu.make_async_copy(feats, full[0].at[:, pl.ds(first_tile, tiles)], own_sem)
    own_copy.start()
    for i in range(2):
        far_copy(i, 0).start()
    for h in range(chunks):
        for d in range(group):
            raw_copy(((slot + d) % group) * chunks + h).start()
    for l in range(layers):
        for i in range(4):
            if l > 0 or i > 1:
                far_copy(i, l).start()

    barrier = pltpu.get_barrier_semaphore()
    for d in range(1, group):
        pl.semaphore_signal(barrier, inc=1, device_id=(base + (slot + d) % group, core), device_id_type=MESH)
    for q in range(1, verts):
        pl.semaphore_signal(barrier, inc=1, device_id=(me, (core + q) % verts), device_id_type=MESH)

    @pl.when(plane > 0)
    def _():
        pl.semaphore_signal(barrier, inc=1, device_id=(me - group, core), device_id_type=MESH)

    @pl.when(plane < groups - 1)
    def _():
        pl.semaphore_signal(barrier, inc=1, device_id=(me + group, core), device_id_type=MESH)

    ahead = jnp.where(plane < groups - 1, 1, 0)
    behind = jnp.where(plane > 0, 1, 0)
    pl.semaphore_wait(barrier, group - 1 + verts - 1 + ahead + behind)

    def first_copy(q):
        return pltpu.make_async_remote_copy(
            src_ref=feats,
            dst_ref=full[0].at[:, pl.ds(first_tile, tiles)],
            send_sem=first_send.at[q],
            recv_sem=first_recv.at[q],
            device_id=(me, (core + q) % verts),
            device_id_type=MESH,
        )

    for q in range(1, verts):
        first_copy(q).start()

    @pl.when(plane == 0)
    def _():
        for l in range(layers):
            for h in range(pieces):
                window[l, h, 0:held] = jnp.zeros((held, rows, width), jnp.bfloat16)

    own_copy.wait()
    for q in range(1, verts):
        first_copy(q).wait_recv()

    def a_copy(l, h, d):
        return pltpu.make_async_remote_copy(
            src_ref=sent_graph.at[l, h, d],
            dst_ref=window.at[l, h, pl.ds(held + slot * snaps, snaps)],
            send_sem=a_send.at[l, h, d],
            recv_sem=a_recv.at[l, h, d],
            device_id=(base + (slot + d) % group, core),
            device_id_type=MESH,
        )

    def z_part(l, h, d, origin, skip):
        return pltpu.make_async_remote_copy(
            src_ref=window.at[l, h, pl.ds(held + origin * snaps + skip, snaps - skip)],
            dst_ref=window.at[l, h, pl.ds(origin * snaps + skip, snaps - skip)],
            send_sem=z_send.at[l, h, d],
            recv_sem=z_recv.at[l, h, d],
            device_id=(jnp.minimum(me + group, owners - 1), core),
            device_id_type=MESH,
        )

    def z_do(l, h, d, act):
        origin = (slot + group - d) % group
        if unused == 0:
            act(z_part(l, h, d, origin, 0))
            return

        @pl.when(origin == 0)
        def _():
            act(z_part(l, h, d, 0, unused))

        @pl.when(origin > 0)
        def _():
            act(z_part(l, h, d, origin, 0))

    def spot(l, owner, h):
        target = out if l == layers - 1 else full[l + 1]
        first = 0 if l == layers - 1 else first_tile
        return target.at[:, first + owner * chunks + h // parts, pl.ds((h % parts) * rows, rows)]

    def b_copy(l, h, d):
        return pltpu.make_async_remote_copy(
            src_ref=sent_time.at[l, h, d],
            dst_ref=spot(l, slot, h),
            send_sem=b_send.at[l, h, d],
            recv_sem=b_recv.at[l, h, d],
            device_id=(base + (slot + d) % group, core),
            device_id_type=MESH,
        )

    def v_copy(l, h, d, q):
        piece = spot(l, (slot + group - d) % group, h)
        return pltpu.make_async_remote_copy(
            src_ref=piece,
            dst_ref=piece,
            send_sem=v_send.at[l, h, d, q],
            recv_sem=v_recv.at[l, h, d, q],
            device_id=(me, (core + q) % verts),
            device_id_type=MESH,
        )

    def hand_on(l, h, d):
        @pl.when(plane < groups - 1)
        def _():
            z_do(l, h, d, lambda copy: copy.start())

    def share(l, h, d):
        if l < layers - 1:
            for q in range(1, verts):
                v_copy(l, h, d, q).start()

    for l in range(layers):
        for i in range(2):
            far_copy(i, l).wait()

        def graph_step(h, d):
            r = ((slot + d) % group) * chunks + h
            if l == 0:
                raw_copy(r).wait()
            sums = []
            for t in range(snaps):
                if l == 0:
                    block = jnp.concatenate(
                        [raw[t, r, k].astype(jnp.float32).astype(jnp.bfloat16) for k in range(picks)], axis=1
                    )
                    blocks[t, r] = block
                else:
                    block = blocks[t, r]
                picked = jnp.concatenate([full[l][t, cols[t, r, k]] for k in range(picks)], axis=0)
                sums.append(jnp.dot(block, picked, preferred_element_type=jnp.float32))
            summed = jnp.concatenate(sums, axis=0)
            branch = mlp(normalise(summed, graph_gain[l:l + 1]), graph_up[l], graph_down[l])
            state = full[l][:, first_tile + r].astype(jnp.float32)
            result = (state + branch.reshape(snaps, tile, width)).astype(jnp.bfloat16)

            for p in range(parts):
                part = result[:, p * rows:(p + 1) * rows]
                if d == 0:
                    window[l, h * parts + p, pl.ds(held + slot * snaps, snaps)] = part
                    hand_on(l, h * parts + p, d)
                else:
                    sent_graph[l, h * parts + p, d] = part
                    a_copy(l, h * parts + p, d).start()

        order = [(h, d) for h in range(chunks) for d in range(1, group)]
        for h in range(chunks):
            order.insert(2 * h + 1, (h, 0))
        for h, d in order:
            graph_step(h, d)
            if h > 0 and d > 0:
                for p in range(parts):
                    a_copy(l, (h - 1) * parts + p, d).wait_recv()
                    hand_on(l, (h - 1) * parts + p, d)
        for p in range(parts):
            for d in range(1, group):
                a_copy(l, pieces - parts + p, d).wait_recv()
                hand_on(l, pieces - parts + p, d)
        for i in range(2, 4):
            far_copy(i, l).wait()

        def time_step(h, first):
            if first == 0:

                @pl.when(plane > 0)
                def _():
                    for e in range(group):
                        z_do(l, h, e, lambda copy: copy.wait_recv())

            mixes, states = [], []
            for c in range(pair):
                owner = (slot + first + c + 1) % group
                for t in range(snaps):
                    newest = held + owner * snaps + t
                    mixed = lag_mix[l, 0:1] * window[l, h, newest].astype(jnp.float32)
                    for m in range(1, lags):
                        mixed = mixed + lag_mix[l, m:m + 1] * window[l, h, newest - m].astype(jnp.float32)
                    mixes.append(mixed)
                    states.append(window[l, h, newest].astype(jnp.float32))
            branch = mlp(normalise(jnp.concatenate(mixes, axis=0), time_gain[l:l + 1]), time_up[l], time_down[l])
            result = (jnp.concatenate(states, axis=0) + branch).astype(jnp.bfloat16)
            result = result.reshape(pair, snaps, rows, width)

            for c in range(pair):
                d = (first + c + 1) % group

                def keep(c=c, d=d):
                    spot(l, slot, h)[...] = result[c]
                    share(l, h, d)

                def send(c=c, d=d):
                    sent_time[l, h, d] = result[c]
                    b_copy(l, h, d).start()

                keep() if d == 0 else send()

        for h in range(pieces):
            for first in range(0, group, pair):
                time_step(h, first)
        for h in range(pieces):
            for d in range(1, group):
                b_copy(l, h, d).wait_recv()
                share(l, h, d)
        if l < layers - 1:
            for h in range(pieces):
                for d in range(group):
                    for q in range(1, verts):
                        v_copy(l, h, d, q).wait_recv()

    for q in range(1, verts):
        first_copy(q).wait_send()
    for l in range(layers):
        for h in range(pieces):
            for d in range(1, group):
                a_copy(l, h, d).wait_send()
                b_copy(l, h, d).wait_send()
            for d in range(group):
                if l < layers - 1:
                    for q in range(1, verts):
                        v_copy(l, h, d, q).wait_send()

                @pl.when(plane < groups - 1)
                def _():
                    z_do(l, h, d, lambda copy: copy.wait_send())


def on_device(owners, verts, features, tile_cols, tile_weights, graph_gain, graph_up, graph_down, lag_mix, time_gain, time_up, time_down):
    snaps, vert_dev, width = features.shape
    _, tiles, picks, tile, _ = tile_weights.shape
    layers, lags = lag_mix.shape[0], lag_mix.shape[1]
    group = -(-(lags - 1) // snaps)
    while owners % group or tiles % group:
        group += 1
    rows = tile
    pieces = tiles // group
    held = group * snaps
    vmem = pl.BlockSpec(memory_space=pltpu.VMEM)
    far = pl.BlockSpec(memory_space=pl.ANY)
    bf16 = jnp.bfloat16
    dma = pltpu.SemaphoreType.DMA
    result = pl.pallas_call(
        functools.partial(kernel, owners, verts, group),
        out_shape=jax.ShapeDtypeStruct((snaps, tiles, tile, width), bf16),
        in_specs=[far, pl.BlockSpec(memory_space=pltpu.SMEM), far, vmem, vmem, vmem] + [far] * 4,
        out_specs=vmem,
        scratch_shapes=[pltpu.VMEM((snaps, verts * tiles, tile, width), bf16)] * layers + [
            pltpu.VMEM((snaps, tiles, picks, tile, tile), jnp.int32),
            pltpu.VMEM((snaps, tiles, tile, picks * tile), bf16),
            pltpu.VMEM((layers, pieces, group, snaps, rows, width), bf16),
            pltpu.VMEM((layers, pieces, 2 * held, rows, width), bf16),
            pltpu.VMEM((layers, pieces, group, snaps, rows, width), bf16),
            pltpu.VMEM(graph_up.shape, bf16),
            pltpu.VMEM(graph_down.shape, bf16),
            pltpu.VMEM(time_up.shape, bf16),
            pltpu.VMEM(time_down.shape, bf16),
            dma,
            dma((4, layers)),
            dma((tiles,)),
            dma((verts,)),
            dma((verts,)),
        ] + [dma((layers, pieces, group))] * 6 + [dma((layers, pieces, group, verts))] * 2,
        compiler_params=pltpu.CompilerParams(
            collective_id=0, has_side_effects=True, vmem_limit_bytes=60 * 1024 * 1024
        ),
    )(
        features.reshape(snaps, tiles, tile, width), tile_cols, tile_weights,
        graph_gain, lag_mix, time_gain, graph_up, graph_down, time_up, time_down,
    )
    return result.reshape(features.shape)


def solution(mesh):
    return jax.shard_map(
        functools.partial(on_device, mesh.shape["snap"], mesh.shape["vert"]),
        mesh=mesh,
        in_specs=(
            P("snap", "vert", None),
            P("snap", "vert", None),
            P("snap", "vert", None, None, None),
        ) + (P(),) * 7,
        out_specs=P("snap", "vert", None),
        check_vma=False,
    )
```
